32 devices in a mesh: dp: 8 (over z, x), tensor: 4 (over y, core).
Axes of the slice: x: 2, y: 2, z: 4, core: 2. Of those that a mesh axis runs over, the one named last changes fastest.
Arguments:
- tokens: bfloat16 [3072, 2048], P('dp', 'tensor'), may hold values from -6 to 6
- partner_bits: int32 [4, 2], replicated, may hold values from 0 to 1, as said below
- w_up: bfloat16 [4, 3, 512, 1024], P('tensor', None, 'dp'), may hold values from -0.15625 to 0.15625
- w_down: bfloat16 [4, 3, 1024, 512], P('tensor', None, 'dp'), may hold values from -0.109375 to 0.109375
Outputs:
- mixed: bfloat16 [3072, 2048], P('dp', 'tensor')
The draws below stay inside these ranges and needn't reach their ends.
Inputs may be any that keep to these rules, and one draw needn't show every extreme that they name: Each row of partner_bits lists each of 0 to 1 exactly once.
All inputs are finite; a program needn't handle non-finite values.
Results may differ from the reference program's by a relative error of at most 0.0057.
Values may be sent and summed in bfloat16 or wider, within the bound.
A program may use at most 64 MiB of HBM per device.

```python
import jax
import jax.numpy as jnp
from jax import lax

D_BLK = 512
FF_BLK = 1024
NB = 4
LINKS = 2
D = 2048
TOKENS = 3072


def draw_partner_bits(key, part):
    scores = jax.random.randint(key, (NB, LINKS), 0, 1 << 20) * LINKS + jnp.arange(LINKS, dtype=jnp.int32)[None, :]
    return jnp.argsort(scores, axis=1).astype(jnp.int32)


def shard_levels(own_key, extent, cuts, smallest, largest):
    def one(axis_at, blocks):
        steps = jax.random.uniform(jax.random.fold_in(jax.random.fold_in(own_key, 6), axis_at), (blocks,), jnp.float32, smallest / len(cuts), largest / len(cuts))
        return jnp.repeat(jnp.exp(steps), extent[axis_at] // blocks).reshape((-1,) + (1,) * (len(extent) - axis_at - 1))

    loudness = one(*cuts[0])
    for cut in cuts[1:]:
        loudness = loudness * one(*cut)
    return loudness


def bell_draw(own_key, extent, spread, bound, split=(), kind=jnp.bfloat16):
    values = spread * jax.random.normal(own_key, extent, jnp.float32)
    if split:
        values = values * shard_levels(own_key, extent, split, -0.22, 0.18)
    return jnp.clip(values, -bound, bound).astype(kind)


def setup_inputs(seed: int = 0) -> dict:
    key_of = jax.random.split(jax.random.key(seed), 5)
    return {
        "tokens": bell_draw(key_of[0], (TOKENS, D), 1.0, 6.0, ((0, 8), (1, 4))),
        "partner_bits": draw_partner_bits(jax.random.fold_in(key_of[4], 71), 0),
        "w_up": bell_draw(key_of[2], (NB, LINKS + 1, D_BLK, FF_BLK), ((LINKS + 1) * D_BLK) ** -0.5, 0.15625, ((0, 4), (2, 8))),
        "w_down": bell_draw(key_of[3], (NB, LINKS + 1, FF_BLK, D_BLK), ((LINKS + 1) * FF_BLK) ** -0.5, 0.109375, ((0, 4), (2, 8))),
    }


def reference(tokens, partner_bits, w_up, w_down):
    blocks = tokens.reshape(TOKENS, NB, D_BLK)
    rows = jnp.arange(NB, dtype=jnp.int32)
    shifted = jnp.left_shift(jnp.ones_like(partner_bits), partner_bits)
    link = jnp.concatenate([rows[:, None], jnp.bitwise_xor(rows[:, None], shifted)], axis=1).astype(jnp.int32)

    def one_block(total, j):
        sel = link[j]
        inputs = jnp.take(blocks, sel, axis=1).astype(jnp.float32)
        up_w = w_up[j].astype(jnp.float32)
        pre = jnp.einsum("tsd,sdf->tf", inputs, up_w, precision=lax.Precision.HIGHEST)
        hidden = jax.nn.gelu(pre, approximate=True).astype(jnp.bfloat16)
        down_w = w_down[j].astype(jnp.float32)
        terms = jnp.einsum("tf,sfd->std", hidden.astype(jnp.float32), down_w, precision=lax.Precision.HIGHEST)
        terms = terms.astype(jnp.bfloat16).astype(jnp.float32)
        total = total.at[sel].add(terms)
        return total, None

    start = jnp.zeros((NB, TOKENS, D_BLK), jnp.float32)
    total, unused = lax.scan(one_block, start, jnp.arange(NB, dtype=jnp.int32))
    return jnp.transpose(total, (1, 0, 2)).reshape(TOKENS, D).astype(jnp.bfloat16)
```

```python
import functools

import jax
import jax.numpy as jnp
from jax import lax
from jax.experimental import pallas as pl
from jax.experimental.pallas import tpu as pltpu
from jax.sharding import PartitionSpec as P

MESH = pl.DeviceIdType.MESH
OWN_CHUNKS = 2


def item_list(slots, width):
    items = [("up", 0, 0, 0), ("up", 1, 0, 0)]
    for slot in range(slots - 1, 0, -1):
        items.append(("down", slot, 0, width))
    part = width // OWN_CHUNKS
    for chunk in range(OWN_CHUNKS):
        items.append(("down", 0, chunk * part, part))
    return items


def kernel(
    nz, items, tok_ref, up_ref, down_ref, out_ref,
    tok, up, down, hid, stage, landed, own,
    line_send, line_recv, local_sem, side_send, side_recv,
    tok_send, tok_recv, term_send, term_recv,
):
    slots = tok.shape[0]
    rows_up, rows_down = up_ref.shape[2], down_ref.shape[1]
    me, rank = lax.axis_index("dp"), lax.axis_index("tensor")
    z, x = me // 2, me % 2
    other = z * 2 + (1 - x)
    partner = [rank]
    for bit in range(slots - 1):
        partner.append(rank + (1 - 2 * ((rank // (1 << bit)) % 2)) * (1 << bit))

    barrier = pltpu.get_barrier_semaphore()
    greeted = [((((z + 1) % nz) * 2 + x), rank), (((z + nz - 1) % nz) * 2 + x, rank), (other, rank)]
    for slot in range(1, slots):
        greeted += [(me, partner[slot]), (other, partner[slot])]
    for device in greeted:
        pl.semaphore_signal(barrier, inc=1, device_id=device, device_id_type=MESH)
    pl.semaphore_wait(barrier, len(greeted))

    def up_rows(at_z, at_x):
        return up.at[:, pl.ds(pl.multiple_of((at_z * 2 + at_x) * rows_up, rows_up), rows_up), :]

    def place(item, at_z):
        kind, which, first, width = item
        if kind == "up":
            return up_rows(at_z, x if which == 0 else 1 - x)
        row = pl.multiple_of(at_z * rows_down, rows_down)
        return down.at[which, pl.ds(row, rows_down), pl.ds(first, width)]

    def source(item, hop, at_z):
        kind, which, first, width = item
        if hop > 1 or (kind == "up" and which == 1):
            return place(item, at_z)
        if kind == "up":
            return up_ref.at[x]
        return down_ref.at[which, :, pl.ds(first, width)]

    def line(i, hop, way):
        sign = 1 - 2 * way
        origin = z - sign * (hop - 1)
        return pltpu.make_async_remote_copy(
            src_ref=source(items[i], hop, origin),
            dst_ref=place(items[i], origin),
            send_sem=line_send.at[i, way, hop - 1],
            recv_sem=line_recv.at[i, way, hop - 1],
            device_id=((z + sign) * 2 + x, rank),
            device_id_type=MESH,
        )

    def sends(hop, way):
        if way == 0:
            return jnp.logical_and(z - (hop - 1) >= 0, z < nz - 1)
        return jnp.logical_and(z + (hop - 1) < nz, z > 0)

    def receives(hop, way):
        return z - hop >= 0 if way == 0 else z + hop < nz

    def send(i, hop):
        for way in (0, 1):
            @pl.when(sends(hop, way))
            def _():
                line(i, hop, way).start()

    def sent(i, hop):
        for way in (0, 1):
            @pl.when(sends(hop, way))
            def _():
                line(i, hop, way).wait_send()

    def arrive(i, hop):
        for way in (0, 1):
            @pl.when(receives(hop, way))
            def _():
                origin = z - (1 - 2 * way) * hop
                pltpu.make_async_remote_copy(
                    src_ref=place(items[i], origin),
                    dst_ref=place(items[i], origin),
                    send_sem=line_send.at[i, way, hop - 1],
                    recv_sem=line_recv.at[i, way, hop - 1],
                    device_id=(me, rank),
                    device_id_type=MESH,
                ).wait_recv()

    def side(dst_x):
        return pltpu.make_async_remote_copy(
            src_ref=up_ref.at[1 - x], dst_ref=up_rows(z, dst_x),
            send_sem=side_send, recv_sem=side_recv,
            device_id=(other, rank), device_id_type=MESH,
        )

    def token_copy(slot, half):
        at = x if half == 0 else 1 - x
        src = tok_ref if half == 0 else tok.at[0, at]
        return pltpu.make_async_remote_copy(
            src_ref=src, dst_ref=tok.at[slot, at],
            send_sem=tok_send.at[slot, half], recv_sem=tok_recv.at[slot, half],
            device_id=(me, partner[slot]), device_id_type=MESH,
        )

    def token_side():
        return pltpu.make_async_remote_copy(
            src_ref=tok_ref, dst_ref=tok.at[0, x],
            send_sem=tok_send.at[0, 0], recv_sem=tok_recv.at[0, 0],
            device_id=(other, rank), device_id_type=MESH,
        )

    def term_copy(i, far):
        unused, slot, first, width = items[i]
        columns = pl.ds(first, width)
        return pltpu.make_async_remote_copy(
            src_ref=stage.at[slot, 1 - x if far else x, :, columns],
            dst_ref=landed.at[slot, x, :, columns],
            send_sem=term_send.at[i, far], recv_sem=term_recv.at[i, far],
            device_id=(other if far else me, partner[slot]), device_id_type=MESH,
        )

    last = nz - 1
    send(0, 1)
    side(x).start()
    token_side().start()
    for slot in range(slots - 1, 0, -1):
        token_copy(slot, 0).start()
    mine = [
        pltpu.make_async_copy(tok_ref, tok.at[0, x], local_sem.at[0]),
        pltpu.make_async_copy(up_ref.at[x], up_rows(z, x), local_sem.at[1]),
        pltpu.make_async_copy(
            down_ref, down.at[:, pl.ds(pl.multiple_of(z * rows_down, rows_down), rows_down), :], local_sem.at[2]
        ),
    ]
    for copy in mine:
        copy.start()

    def make_hidden():
        for copy in mine:
            copy.wait()
        for slot in range(1, slots):
            for half in (0, 1):
                token_copy(slot, half).wait_recv()

        def one(half, carry):
            pre = jnp.dot(tok[0, half], up[0], preferred_element_type=jnp.float32)
            for slot in range(1, slots):
                pre += jnp.dot(tok[slot, half], up[slot], preferred_element_type=jnp.float32)
            hid[half] = jax.nn.gelu(pre, approximate=True).astype(hid.dtype)
            return carry

        lax.fori_loop(0, 2, one, 0)

    def make_terms(i):
        unused, slot, first, width = items[i]
        columns = slice(first, first + width)

        def term(half):
            return jnp.dot(hid[half], down[slot, :, columns], preferred_element_type=jnp.float32)

        stage[slot, 1 - x, :, columns] = term(1 - x).astype(stage.dtype)
        term_copy(i, 1).start()
        if slot == 0:
            own[:, columns] = term(x)
        else:
            stage[slot, x, :, columns] = term(x).astype(stage.dtype)
            term_copy(i, 0).start()

    count = len(items)
    for step in range(count + last):
        for hop in range(1, nz + 1):
            i = step - (hop - 1)
            if not 0 <= i < count:
                continue
            if hop > 1:
                arrive(i, hop - 1)
            elif i == 1:
                side(1 - x).wait_recv()
            if hop < nz:
                if (i, hop) != (0, 1):
                    send(i, hop)
        if step == 1:
            token_side().wait_recv()
            for slot in range(slots - 1, 0, -1):
                token_copy(slot, 1).start()
        i = step - last
        if i == 1:
            make_hidden()
        if i > 1:
            make_terms(i)

    for i in range(2, count):
        unused, slot, first, width = items[i]
        term_copy(i, 1).wait_recv()
        if slot:
            term_copy(i, 0).wait_recv()
            continue
        columns = slice(first, first + width)
        total = own[:, columns] + landed[0, 1 - x, :, columns].astype(jnp.float32)
        for slot in range(1, slots):
            for half in (0, 1):
                total += landed[slot, half, :, columns].astype(jnp.float32)
        out_ref[:, columns] = total.astype(out_ref.dtype)

    side(x).wait_send()
    token_side().wait_send()
    for slot in range(1, slots):
        for half in (0, 1):
            token_copy(slot, half).wait_send()
    for i in range(count):
        for hop in range(1, nz):
            sent(i, hop)
        if i > 1:
            term_copy(i, 1).wait_send()
            if items[i][1]:
                term_copy(i, 0).wait_send()


def on_device(tokens, partner_bits, w_up, w_down):
    dp, rank = lax.axis_size("dp"), lax.axis_index("tensor")
    nz = dp // 2
    slots = w_up.shape[1]
    rows, width = tokens.shape
    rows_up, hidden = w_up.shape[2], w_up.shape[3]
    rows_down = w_down.shape[2]
    half = hidden // 2
    my_bits = lax.dynamic_slice_in_dim(partner_bits, rank, 1, 0)[0]
    order = jnp.sum(
        (my_bits[None, :] == jnp.arange(slots - 1, dtype=jnp.int32)[:, None])
        * jnp.arange(1, slots, dtype=jnp.int32)[None, :], axis=1,
    )

    def by_bit(weights):
        picked = [weights[0]]
        for bit in range(slots - 1):
            choice = weights[1]
            for slot in range(2, slots):
                choice = jnp.where(order[bit] == slot, weights[slot], choice)
            picked.append(choice)
        return jnp.stack(picked)

    up = by_bit(w_up[0]).reshape(slots, rows_up, nz, 2, hidden // dp)
    up = up.transpose(3, 0, 1, 2, 4).reshape(2, slots, rows_up, half)
    down = by_bit(w_down[0])
    items = item_list(slots, width)
    count = len(items)
    kind = tokens.dtype
    dma = pltpu.SemaphoreType.DMA
    return pl.pallas_call(
        functools.partial(kernel, nz, items),
        out_shape=jax.ShapeDtypeStruct((rows, width), kind),
        in_specs=[pl.BlockSpec(memory_space=pltpu.VMEM)] * 3,
        out_specs=pl.BlockSpec(memory_space=pltpu.VMEM),
        scratch_shapes=[
            pltpu.VMEM((slots, 2, rows, width), kind),
            pltpu.VMEM((slots, width, half), kind),
            pltpu.VMEM((slots, half, width), kind),
            pltpu.VMEM((2, rows, half), kind),
            pltpu.VMEM((slots, 2, rows, width), kind),
            pltpu.VMEM((slots, 2, rows, width), kind),
            pltpu.VMEM((rows, width), jnp.float32),
            dma((count, 2, nz - 1)),
            dma((count, 2, nz - 1)),
            dma((3,)),
            dma,
            dma,
            dma((slots, 2)),
            dma((slots, 2)),
            dma((count, 2)),
            dma((count, 2)),
        ],
        compiler_params=pltpu.CompilerParams(
            collective_id=0, has_side_effects=True, vmem_limit_bytes=48 << 20
        ),
    )(tokens, up, down)


def solution(mesh):
    in_specs = (
        P("dp", "tensor"),
        P(),
        P("tensor", None, "dp", None),
        P("tensor", None, "dp", None),
    )
    return jax.shard_map(
        on_device, mesh=mesh, in_specs=in_specs, out_specs=P("dp", "tensor"), check_vma=False
    )
```

```python
import functools

import jax
import jax.numpy as jnp
from jax import lax
from jax.experimental import pallas as pl
from jax.experimental.pallas import tpu as pltpu
from jax.sharding import PartitionSpec as P

MESH = pl.DeviceIdType.MESH
OWN_CHUNKS = 2


def item_list(slots, width):
    items = [("up", 0, 0, 0), ("up", 1, 0, 0)]
    for slot in range(slots - 1, 0, -1):
        items.append(("down", slot, 0, width))
    part = width // OWN_CHUNKS
    for chunk in range(OWN_CHUNKS):
        items.append(("down", 0, chunk * part, part))
    return items


def kernel(
    nz, items, bits_ref, tok_ref, up_raw, down_raw, out_ref,
    tok, up, down, hid, stage, landed, own, up_in, down_in, up_away,
    line_send, line_recv, local_sem, side_send, side_recv,
    tok_send, tok_recv, term_send, term_recv,
):
    slots = tok.shape[0]
    rows_up, rows_down, strip = up_raw.shape[2], down_raw.shape[2], up_raw.shape[3] // (2 * nz)
    me, rank = lax.axis_index("dp"), lax.axis_index("tensor")
    z, x = me // 2, me % 2
    other = z * 2 + (1 - x)
    partner = [rank]
    for bit in range(slots - 1):
        partner.append(rank + (1 - 2 * ((rank // (1 << bit)) % 2)) * (1 << bit))

    fetch_up = pltpu.make_async_copy(up_raw.at[0], up_in, local_sem.at[0])
    fetch_down = pltpu.make_async_copy(down_raw.at[0], down_in, local_sem.at[1])
    mine = pltpu.make_async_copy(tok_ref, tok.at[0, x], local_sem.at[2])
    fetch_up.start()
    fetch_down.start()
    mine.start()
    barrier = pltpu.get_barrier_semaphore()
    greeted = [((((z + 1) % nz) * 2 + x), rank), (((z + nz - 1) % nz) * 2 + x, rank), (other, rank)]
    for slot in range(1, slots):
        greeted += [(me, partner[slot]), (other, partner[slot])]
    for device in greeted:
        pl.semaphore_signal(barrier, inc=1, device_id=device, device_id_type=MESH)
    bits = [jnp.clip(bits_ref[rank, slot], 0, slots - 2) for slot in range(slots - 1)]
    fetch_up.wait()
    own_row = pl.multiple_of((z * 2 + x) * rows_up, rows_up)
    for strip_z in range(nz):
        columns = slice(strip_z * strip, (strip_z + 1) * strip)
        even, odd = (
            up_in[:, :, (2 * strip_z + at) * strip:(2 * strip_z + at + 1) * strip] for at in (0, 1)
        )
        up_away[:, :, columns] = jnp.where(x == 0, odd, even)
        up[:, pl.ds(own_row, rows_up), columns] = jnp.where(x == 0, even, odd)
    fetch_down.wait()
    down_row = pl.multiple_of(z * rows_down, rows_down)
    for bit in range(slots - 1):
        pick = jnp.int32(0)
        for slot in range(slots - 1):
            pick += jnp.where(bits[slot] == bit, slot + 1, 0)
        down[bit + 1, pl.ds(down_row, rows_down), :] = down_in[jnp.minimum(pick, slots - 1)]
    down[0, pl.ds(down_row, rows_down), :] = down_in[0]
    pl.semaphore_wait(barrier, len(greeted))

    def up_rows(at_z, at_x):
        return up.at[:, pl.ds(pl.multiple_of((at_z * 2 + at_x) * rows_up, rows_up), rows_up), :]

    def place(item, at_z):
        kind, which, first, width = item
        if kind == "up":
            return up_rows(at_z, x if which == 0 else 1 - x)
        row = pl.multiple_of(at_z * rows_down, rows_down)
        return down.at[which, pl.ds(row, rows_down), pl.ds(first, width)]

    def line(i, hop, way):
        sign = 1 - 2 * way
        origin = z - sign * (hop - 1)
        return pltpu.make_async_remote_copy(
            src_ref=place(items[i], origin),
            dst_ref=place(items[i], origin),
            send_sem=line_send.at[i, way, hop - 1],
            recv_sem=line_recv.at[i, way, hop - 1],
            device_id=((z + sign) * 2 + x, rank),
            device_id_type=MESH,
        )

    def sends(hop, way):
        if way == 0:
            return jnp.logical_and(z - (hop - 1) >= 0, z < nz - 1)
        return jnp.logical_and(z + (hop - 1) < nz, z > 0)

    def receives(hop, way):
        return z - hop >= 0 if way == 0 else z + hop < nz

    def send(i, hop):
        for way in (0, 1):
            @pl.when(sends(hop, way))
            def _():
                line(i, hop, way).start()

    def sent(i, hop):
        for way in (0, 1):
            @pl.when(sends(hop, way))
            def _():
                line(i, hop, way).wait_send()

    def arrive(i, hop):
        for way in (0, 1):
            @pl.when(receives(hop, way))
            def _():
                origin = z - (1 - 2 * way) * hop
                pltpu.make_async_remote_copy(
                    src_ref=place(items[i], origin),
                    dst_ref=place(items[i], origin),
                    send_sem=line_send.at[i, way, hop - 1],
                    recv_sem=line_recv.at[i, way, hop - 1],
                    device_id=(me, rank),
                    device_id_type=MESH,
                ).wait_recv()

    def side(dst_x):
        return pltpu.make_async_remote_copy(
            src_ref=up_away, dst_ref=up_rows(z, dst_x),
            send_sem=side_send, recv_sem=side_recv,
            device_id=(other, rank), device_id_type=MESH,
        )

    def token_copy(slot, half):
        at = x if half == 0 else 1 - x
        src = tok_ref if half == 0 else tok.at[0, at]
        return pltpu.make_async_remote_copy(
            src_ref=src, dst_ref=tok.at[slot, at],
            send_sem=tok_send.at[slot, half], recv_sem=tok_recv.at[slot, half],
            device_id=(me, partner[slot]), device_id_type=MESH,
        )

    def token_side():
        return pltpu.make_async_remote_copy(
            src_ref=tok_ref, dst_ref=tok.at[0, x],
            send_sem=tok_send.at[0, 0], recv_sem=tok_recv.at[0, 0],
            device_id=(other, rank), device_id_type=MESH,
        )

    def term_copy(i, far):
        unused, slot, first, width = items[i]
        columns = pl.ds(first, width)
        return pltpu.make_async_remote_copy(
            src_ref=stage.at[slot, 1 - x if far else x, :, columns],
            dst_ref=landed.at[slot, x, :, columns],
            send_sem=term_send.at[i, far], recv_sem=term_recv.at[i, far],
            device_id=(other if far else me, partner[slot]), device_id_type=MESH,
        )

    last = nz - 1
    send(0, 1)
    side(x).start()
    token_side().start()
    for slot in range(slots - 1, 0, -1):
        token_copy(slot, 0).start()
    def make_hidden():
        mine.wait()
        for slot in range(1, slots):
            for half in (0, 1):
                token_copy(slot, half).wait_recv()

        def one(half, carry):
            pre = jnp.dot(tok[0, half], up[0], preferred_element_type=jnp.float32)
            for slot in range(1, slots):
                pre += jnp.dot(tok[1 + bits[slot - 1], half], up[slot], preferred_element_type=jnp.float32)
            hid[half] = jax.nn.gelu(pre, approximate=True).astype(hid.dtype)
            return carry

        lax.fori_loop(0, 2, one, 0)

    def make_terms(i):
        unused, slot, first, width = items[i]
        columns = slice(first, first + width)

        def term(half):
            return jnp.dot(hid[half], down[slot, :, columns], preferred_element_type=jnp.float32)

        stage[slot, 1 - x, :, columns] = term(1 - x).astype(stage.dtype)
        term_copy(i, 1).start()
        if slot == 0:
            own[:, columns] = term(x)
        else:
            stage[slot, x, :, columns] = term(x).astype(stage.dtype)
            term_copy(i, 0).start()

    count = len(items)
    for step in range(count + last):
        for hop in range(1, nz + 1):
            i = step - (hop - 1)
            if not 0 <= i < count:
                continue
            if hop > 1:
                arrive(i, hop - 1)
            elif i == 1:
                side(1 - x).wait_recv()
            if hop < nz:
                if (i, hop) != (0, 1):
                    send(i, hop)
        if step == 1:
            token_side().wait_recv()
            for slot in range(slots - 1, 0, -1):
                token_copy(slot, 1).start()
        i = step - last
        if i == 1:
            make_hidden()
        if i > 1:
            make_terms(i)

    for i in range(2, count):
        unused, slot, first, width = items[i]
        term_copy(i, 1).wait_recv()
        if slot:
            term_copy(i, 0).wait_recv()
            continue
        columns = slice(first, first + width)
        total = own[:, columns] + landed[0, 1 - x, :, columns].astype(jnp.float32)
        for slot in range(1, slots):
            for half in (0, 1):
                total += landed[slot, half, :, columns].astype(jnp.float32)
        out_ref[:, columns] = total.astype(out_ref.dtype)

    side(x).wait_send()
    token_side().wait_send()
    for slot in range(1, slots):
        for half in (0, 1):
            token_copy(slot, half).wait_send()
    for i in range(count):
        for hop in range(1, nz):
            sent(i, hop)
        if i > 1:
            term_copy(i, 1).wait_send()
            if items[i][1]:
                term_copy(i, 0).wait_send()


def on_device(tokens, partner_bits, w_up, w_down):
    nz = lax.axis_size("dp") // 2
    slots = w_up.shape[1]
    rows, width = tokens.shape
    rows_up, hidden = w_up.shape[2], w_up.shape[3]
    rows_down = w_down.shape[2]
    half = hidden // 2
    items = item_list(slots, width)
    count = len(items)
    kind = tokens.dtype
    dma = pltpu.SemaphoreType.DMA
    return pl.pallas_call(
        functools.partial(kernel, nz, items),
        out_shape=jax.ShapeDtypeStruct((rows, width), kind),
        in_specs=[pl.BlockSpec(memory_space=pltpu.SMEM)] + [pl.BlockSpec(memory_space=pl.ANY)] * 3,
        out_specs=pl.BlockSpec(memory_space=pltpu.VMEM),
        scratch_shapes=[
            pltpu.VMEM((slots, 2, rows, width), kind),
            pltpu.VMEM((slots, width, half), kind),
            pltpu.VMEM((slots, half, width), kind),
            pltpu.VMEM((2, rows, half), kind),
            pltpu.VMEM((slots, 2, rows, width), kind),
            pltpu.VMEM((slots, 2, rows, width), kind),
            pltpu.VMEM((rows, width), jnp.float32),
            pltpu.VMEM(w_up.shape[1:], kind),
            pltpu.VMEM(w_down.shape[1:], kind),
            pltpu.VMEM((slots, rows_up, half), kind),
            dma((count, 2, nz - 1)),
            dma((count, 2, nz - 1)),
            dma((3,)),
            dma,
            dma,
            dma((slots, 2)),
            dma((slots, 2)),
            dma((count, 2)),
            dma((count, 2)),
        ],
        compiler_params=pltpu.CompilerParams(
            collective_id=0, has_side_effects=True, vmem_limit_bytes=67043328
        ),
    )(partner_bits, tokens, w_up, w_down)


def solution(mesh):
    in_specs = (
        P("dp", "tensor"),
        P(),
        P("tensor", None, "dp", None),
        P("tensor", None, "dp", None),
    )
    return jax.shard_map(
        on_device, mesh=mesh, in_specs=in_specs, out_specs=P("dp", "tensor"), check_vma=False
    )
```

```python
import functools

import jax
import jax.numpy as jnp
from jax import lax
from jax.experimental import pallas as pl
from jax.experimental.pallas import tpu as pltpu
from jax.sharding import PartitionSpec as P

MESH = pl.DeviceIdType.MESH
CHUNKS = 2


def item_list(width):
    part = width // CHUNKS
    return [("up", 0, 0), ("up", 1, 0)] + [("down", c * part, part) for c in range(CHUNKS)]


def kernel(
    nz, items, bits_ref, tok_ref, up_raw, down_raw, out_ref,
    tok, up, down, hid, stage, landed, own, up_in, down_in, up_away, down_away,
    line_send, line_recv, local_sem, side_send, side_recv,
    tok_send, tok_recv, down_send, down_recv, hid_send, hid_recv, sum_send, sum_recv,
):
    slots = tok.shape[0]
    rows_up, rows_down, strip = up_raw.shape[2], down_raw.shape[2], up_raw.shape[3] // (2 * nz)
    me, rank = lax.axis_index("dp"), lax.axis_index("tensor")
    z, x = me // 2, me % 2
    other = z * 2 + (1 - x)
    partner = [rank]
    for bit in range(slots - 1):
        partner.append(rank + (1 - 2 * ((rank // (1 << bit)) % 2)) * (1 << bit))

    fetch_up = pltpu.make_async_copy(up_raw.at[0], up_in, local_sem.at[0])
    fetch_down = pltpu.make_async_copy(down_raw.at[0], down_in, local_sem.at[1])
    mine = pltpu.make_async_copy(tok_ref, tok.at[0, x], local_sem.at[2])
    fetch_up.start()
    fetch_down.start()
    mine.start()
    barrier = pltpu.get_barrier_semaphore()
    greeted = [((((z + 1) % nz) * 2 + x), rank), (((z + nz - 1) % nz) * 2 + x, rank), (other, rank)]
    for slot in range(1, slots):
        greeted += [(me, partner[slot]), (other, partner[slot])]
    for device in greeted:
        pl.semaphore_signal(barrier, inc=1, device_id=device, device_id_type=MESH)
    bits = [jnp.clip(bits_ref[slot, rank], 0, slots - 2) for slot in range(slots - 1)]
    fetch_up.wait()
    own_row = pl.multiple_of((z * 2 + x) * rows_up, rows_up)
    for strip_z in range(nz):
        columns = slice(strip_z * strip, (strip_z + 1) * strip)
        even, odd = (
            up_in[:, :, (2 * strip_z + at) * strip:(2 * strip_z + at + 1) * strip] for at in (0, 1)
        )
        up_away[:, :, columns] = jnp.where(x == 0, odd, even)
        up[:, pl.ds(own_row, rows_up), columns] = jnp.where(x == 0, even, odd)
    fetch_down.wait()
    down_row = pl.multiple_of(z * rows_down, rows_down)
    for bit in range(slots - 1):
        pick = jnp.int32(0)
        for slot in range(slots - 1):
            pick += jnp.where(bits[slot] == bit, slot + 1, 0)
        down_away[bit] = down_in[jnp.minimum(pick, slots - 1)]
    down[0, pl.ds(down_row, rows_down), :] = down_in[0]
    pl.semaphore_wait(barrier, len(greeted))

    def up_rows(at_z, at_x):
        return up.at[:, pl.ds(pl.multiple_of((at_z * 2 + at_x) * rows_up, rows_up), rows_up), :]

    def place(item, at_z):
        kind, first, width = item
        if kind == "up":
            return up_rows(at_z, x if first == 0 else 1 - x)
        row = pl.multiple_of(at_z * rows_down, rows_down)
        return down.at[:, pl.ds(row, rows_down), pl.ds(first, width)]

    def line(i, hop, way):
        sign = 1 - 2 * way
        origin = z - sign * (hop - 1)
        return pltpu.make_async_remote_copy(
            src_ref=place(items[i], origin),
            dst_ref=place(items[i], origin),
            send_sem=line_send.at[i, way, hop - 1],
            recv_sem=line_recv.at[i, way, hop - 1],
            device_id=((z + sign) * 2 + x, rank),
            device_id_type=MESH,
        )

    def sends(hop, way):
        if way == 0:
            return jnp.logical_and(z - (hop - 1) >= 0, z < nz - 1)
        return jnp.logical_and(z + (hop - 1) < nz, z > 0)

    def receives(hop, way):
        return z - hop >= 0 if way == 0 else z + hop < nz

    def send(i, hop):
        for way in (0, 1):
            @pl.when(sends(hop, way))
            def _():
                line(i, hop, way).start()

    def sent(i, hop):
        for way in (0, 1):
            @pl.when(sends(hop, way))
            def _():
                line(i, hop, way).wait_send()

    def arrive(i, hop):
        for way in (0, 1):
            @pl.when(receives(hop, way))
            def _():
                origin = z - (1 - 2 * way) * hop
                pltpu.make_async_remote_copy(
                    src_ref=place(items[i], origin),
                    dst_ref=place(items[i], origin),
                    send_sem=line_send.at[i, way, hop - 1],
                    recv_sem=line_recv.at[i, way, hop - 1],
                    device_id=(me, rank),
                    device_id_type=MESH,
                ).wait_recv()

    def side(dst_x):
        return pltpu.make_async_remote_copy(
            src_ref=up_away, dst_ref=up_rows(z, dst_x),
            send_sem=side_send, recv_sem=side_recv,
            device_id=(other, rank), device_id_type=MESH,
        )

    def token_copy(slot, half):
        at = x if half == 0 else 1 - x
        src = tok_ref if half == 0 else tok.at[0, at]
        return pltpu.make_async_remote_copy(
            src_ref=src, dst_ref=tok.at[slot, at],
            send_sem=tok_send.at[slot, half], recv_sem=tok_recv.at[slot, half],
            device_id=(me, partner[slot]), device_id_type=MESH,
        )

    def token_side():
        return pltpu.make_async_remote_copy(
            src_ref=tok_ref, dst_ref=tok.at[0, x],
            send_sem=tok_send.at[0, 0], recv_sem=tok_recv.at[0, 0],
            device_id=(other, rank), device_id_type=MESH,
        )

    def down_copy(slot):
        return pltpu.make_async_remote_copy(
            src_ref=down_away.at[slot - 1], dst_ref=down.at[slot, pl.ds(down_row, rows_down), :],
            send_sem=down_send.at[slot], recv_sem=down_recv.at[slot],
            device_id=(me, partner[slot]), device_id_type=MESH,
        )

    def hid_copy(slot, far):
        at = 1 - x if far else x
        return pltpu.make_async_remote_copy(
            src_ref=hid.at[0, at], dst_ref=hid.at[slot, at],
            send_sem=hid_send.at[slot, far], recv_sem=hid_recv.at[slot, far],
            device_id=(me, partner[slot]), device_id_type=MESH,
        )

    def sum_copy(i):
        columns = pl.ds(items[i][1], items[i][2])
        return pltpu.make_async_remote_copy(
            src_ref=stage.at[:, columns], dst_ref=landed.at[:, columns],
            send_sem=sum_send.at[i], recv_sem=sum_recv.at[i],
            device_id=(other, rank), device_id_type=MESH,
        )

    send(0, 1)
    side(x).start()
    token_side().start()
    for slot in range(slots - 1, 0, -1):
        token_copy(slot, 0).start()
    for slot in range(slots - 1, 0, -1):
        down_copy(slot).start()
    def make_hidden():
        mine.wait()
        for slot in range(1, slots):
            for half in (0, 1):
                token_copy(slot, half).wait_recv()

        def one(step, carry):
            half = (1 - x) * (1 - step) + x * step
            pre = jnp.dot(tok[0, half], up[0], preferred_element_type=jnp.float32)
            for slot in range(1, slots):
                pre += jnp.dot(tok[1 + bits[slot - 1], half], up[slot], preferred_element_type=jnp.float32)
            hid[0, half] = jax.nn.gelu(pre, approximate=True).astype(hid.dtype)
            return carry

        lax.fori_loop(0, 2, one, 0)
        for far in (1, 0):
            for slot in range(slots - 1, 0, -1):
                hid_copy(slot, far).start()

    def product(at, columns):
        total = jnp.dot(hid[0, at], down[0, :, columns], preferred_element_type=jnp.float32)
        for slot in range(1, slots):
            total += jnp.dot(hid[slot, at], down[slot, :, columns], preferred_element_type=jnp.float32)
        return total

    def make_away(i):
        unused, first, width = items[i]
        columns = slice(first, first + width)
        if first == 0:
            for slot in range(1, slots):
                hid_copy(slot, 1).wait_recv()
        stage[:, columns] = product(1 - x, columns).astype(stage.dtype)
        sum_copy(i).start()

    def complete(i):
        arrive(i, nz - 1)
        if i == 1:
            make_hidden()
        if i > 1:
            make_away(i)

    def first_send(i):
        if i >= count:
            return
        if i == 1:
            side(1 - x).wait_recv()
        if i == 2:
            for slot in range(1, slots):
                down_copy(slot).wait_recv()
        send(i, 1)

    count = len(items)
    for i in range(count):
        first_send(i + 1)
        for hop in range(1, nz):
            if hop < nz - 1:
                arrive(i, hop)
                send(i, hop + 1)
            if hop == 1 and i > 0:
                complete(i - 1)
        if i == 0:
            token_side().wait_recv()
            for slot in range(slots - 1, 0, -1):
                token_copy(slot, 1).start()
    complete(count - 1)
    for slot in range(1, slots):
        hid_copy(slot, 0).wait_recv()
    own[...] = product(x, slice(None))
    for i in range(2, count):
        sum_copy(i).wait_recv()
        columns = slice(items[i][1], items[i][1] + items[i][2])
        out_ref[:, columns] = (own[:, columns] + landed[:, columns].astype(jnp.float32)).astype(out_ref.dtype)

    side(x).wait_send()
    token_side().wait_send()
    for slot in range(1, slots):
        down_copy(slot).wait_send()
        for half in (0, 1):
            token_copy(slot, half).wait_send()
            hid_copy(slot, half).wait_send()
    for i in range(count):
        for hop in range(1, nz):
            sent(i, hop)
        if i > 1:
            sum_copy(i).wait_send()


def on_device(tokens, partner_bits, w_up, w_down):
    nz = lax.axis_size("dp") // 2
    slots = w_up.shape[1]
    rows, width = tokens.shape
    rows_up, hidden = w_up.shape[2], w_up.shape[3]
    rows_down = w_down.shape[2]
    half = hidden // 2
    items = item_list(width)
    count = len(items)
    kind = tokens.dtype
    dma = pltpu.SemaphoreType.DMA
    return pl.pallas_call(
        functools.partial(kernel, nz, items),
        out_shape=jax.ShapeDtypeStruct((rows, width), kind),
        in_specs=[pl.BlockSpec(memory_space=pltpu.SMEM)] + [pl.BlockSpec(memory_space=pl.ANY)] * 3,
        out_specs=pl.BlockSpec(memory_space=pltpu.VMEM),
        scratch_shapes=[
            pltpu.VMEM((slots, 2, rows, width), kind),
            pltpu.VMEM((slots, width, half), kind),
            pltpu.VMEM((slots, half, width), kind),
            pltpu.VMEM((slots, 2, rows, half), kind),
            pltpu.VMEM((rows, width), kind),
            pltpu.VMEM((rows, width), kind),
            pltpu.VMEM((rows, width), jnp.float32),
            pltpu.VMEM(w_up.shape[1:], kind),
            pltpu.VMEM(w_down.shape[1:], kind),
            pltpu.VMEM((slots, rows_up, half), kind),
            pltpu.VMEM((slots - 1,) + w_down.shape[2:], kind),
            dma((count, 2, nz - 1)),
            dma((count, 2, nz - 1)),
            dma((3,)),
            dma,
            dma,
            dma((slots, 2)),
            dma((slots, 2)),
            dma((slots,)),
            dma((slots,)),
            dma((slots, 2)),
            dma((slots, 2)),
            dma((count,)),
            dma((count,)),
        ],
        compiler_params=pltpu.CompilerParams(
            collective_id=0, has_side_effects=True, vmem_limit_bytes=67043328
        ),
    )(partner_bits.T, tokens, w_up, w_down)


def solution(mesh):
    in_specs = (
        P("dp", "tensor"),
        P(),
        P("tensor", None, "dp", None),
        P("tensor", None, "dp", None),
    )
    return jax.shard_map(
        on_device, mesh=mesh, in_specs=in_specs, out_specs=P("dp", "tensor"), check_vma=False
    )
```

```python
import functools

import jax
import jax.numpy as jnp
from jax import lax
from jax.experimental import pallas as pl
from jax.experimental.pallas import tpu as pltpu
from jax.sharding import PartitionSpec as P

MESH = pl.DeviceIdType.MESH
CHUNKS = (2, 4, 4)


def item_list(width):
    items, first = [("up", 0, 0), ("up", 1, 0)], 0
    for share in CHUNKS:
        items.append(("down", first, width // share))
        first += width // share
    return items


def kernel(
    nz, items, bits_ref, tok_ref, up_raw, down_raw, out_ref,
    tok, up, down, hid, stage, landed, own, up_in, down_in, up_away, down_away,
    line_send, line_recv, local_sem, side_send, side_recv,
    tok_send, tok_recv, down_send, down_recv, hid_send, hid_recv, sum_send, sum_recv,
):
    slots = tok.shape[0]
    rows_up, rows_down, strip = up_raw.shape[2], down_raw.shape[2], up_raw.shape[3] // (2 * nz)
    me, rank = lax.axis_index("dp"), lax.axis_index("tensor")
    z, x = me // 2, me % 2
    other = z * 2 + (1 - x)
    partner = [rank]
    for bit in range(slots - 1):
        partner.append(rank + (1 - 2 * ((rank // (1 << bit)) % 2)) * (1 << bit))

    fetch_up = pltpu.make_async_copy(up_raw.at[0], up_in, local_sem.at[0])
    fetch_down = pltpu.make_async_copy(down_raw.at[0], down_in, local_sem.at[1])
    mine = pltpu.make_async_copy(tok_ref, tok.at[0, x], local_sem.at[2])
    fetch_up.start()
    fetch_down.start()
    mine.start()
    barrier = pltpu.get_barrier_semaphore()
    greeted = [((((z + 1) % nz) * 2 + x), rank), (((z + nz - 1) % nz) * 2 + x, rank), (other, rank)]
    for slot in range(1, slots):
        greeted += [(me, partner[slot]), (other, partner[slot])]
    for device in greeted:
        pl.semaphore_signal(barrier, inc=1, device_id=device, device_id_type=MESH)
    down_row = pl.multiple_of(z * rows_down, rows_down)
    bits = [jnp.clip(bits_ref[slot, rank], 0, slots - 2) for slot in range(slots - 1)]
    fetch_up.wait()
    own_row = pl.multiple_of((z * 2 + x) * rows_up, rows_up)
    for strip_z in range(nz):
        columns = slice(strip_z * strip, (strip_z + 1) * strip)
        even, odd = (
            up_in[:, :, (2 * strip_z + at) * strip:(2 * strip_z + at + 1) * strip] for at in (0, 1)
        )
        up_away[:, :, columns] = jnp.where(x == 0, odd, even)
        up[:, pl.ds(own_row, rows_up), columns] = jnp.where(x == 0, even, odd)
    pl.semaphore_wait(barrier, len(greeted))

    def up_rows(at_z, at_x):
        return up.at[:, pl.ds(pl.multiple_of((at_z * 2 + at_x) * rows_up, rows_up), rows_up), :]

    def place(item, at_z):
        kind, first, width = item
        if kind == "up":
            return up_rows(at_z, x if first == 0 else 1 - x)
        row = pl.multiple_of(at_z * rows_down, rows_down)
        return down.at[:, pl.ds(row, rows_down), pl.ds(first, width)]

    def line(i, hop, way):
        sign = 1 - 2 * way
        origin = z - sign * (hop - 1)
        return pltpu.make_async_remote_copy(
            src_ref=place(items[i], origin),
            dst_ref=place(items[i], origin),
            send_sem=line_send.at[i, way, hop - 1],
            recv_sem=line_recv.at[i, way, hop - 1],
            device_id=((z + sign) * 2 + x, rank),
            device_id_type=MESH,
        )

    def sends(hop, way):
        if way == 0:
            return jnp.logical_and(z - (hop - 1) >= 0, z < nz - 1)
        return jnp.logical_and(z + (hop - 1) < nz, z > 0)

    def receives(hop, way):
        return z - hop >= 0 if way == 0 else z + hop < nz

    def send(i, hop):
        for way in (0, 1):
            @pl.when(sends(hop, way))
            def _():
                line(i, hop, way).start()

    def sent(i, hop):
        for way in (0, 1):
            @pl.when(sends(hop, way))
            def _():
                line(i, hop, way).wait_send()

    def arrive(i, hop):
        for way in (0, 1):
            @pl.when(receives(hop, way))
            def _():
                origin = z - (1 - 2 * way) * hop
                pltpu.make_async_remote_copy(
                    src_ref=place(items[i], origin),
                    dst_ref=place(items[i], origin),
                    send_sem=line_send.at[i, way, hop - 1],
                    recv_sem=line_recv.at[i, way, hop - 1],
                    device_id=(me, rank),
                    device_id_type=MESH,
                ).wait_recv()

    def side(dst_x):
        return pltpu.make_async_remote_copy(
            src_ref=up_away, dst_ref=up_rows(z, dst_x),
            send_sem=side_send, recv_sem=side_recv,
            device_id=(other, rank), device_id_type=MESH,
        )

    def token_copy(slot, half):
        at = x if half == 0 else 1 - x
        src = tok_ref if half == 0 else tok.at[0, at]
        return pltpu.make_async_remote_copy(
            src_ref=src, dst_ref=tok.at[slot, at],
            send_sem=tok_send.at[slot, half], recv_sem=tok_recv.at[slot, half],
            device_id=(me, partner[slot]), device_id_type=MESH,
        )

    def token_side():
        return pltpu.make_async_remote_copy(
            src_ref=tok_ref, dst_ref=tok.at[0, x],
            send_sem=tok_send.at[0, 0], recv_sem=tok_recv.at[0, 0],
            device_id=(other, rank), device_id_type=MESH,
        )

    def down_copy(slot):
        return pltpu.make_async_remote_copy(
            src_ref=down_away.at[slot - 1], dst_ref=down.at[slot, pl.ds(down_row, rows_down), :],
            send_sem=down_send.at[slot], recv_sem=down_recv.at[slot],
            device_id=(me, partner[slot]), device_id_type=MESH,
        )

    def hid_copy(slot, far):
        at = 1 - x if far else x
        return pltpu.make_async_remote_copy(
            src_ref=hid.at[0, at], dst_ref=hid.at[slot, at],
            send_sem=hid_send.at[slot, far], recv_sem=hid_recv.at[slot, far],
            device_id=(me, partner[slot]), device_id_type=MESH,
        )

    def sum_copy(i):
        columns = pl.ds(items[i][1], items[i][2])
        return pltpu.make_async_remote_copy(
            src_ref=stage.at[:, columns], dst_ref=landed.at[:, columns],
            send_sem=sum_send.at[i], recv_sem=sum_recv.at[i],
            device_id=(other, rank), device_id_type=MESH,
        )

    send(0, 1)
    side(x).start()
    token_side().start()
    for slot in range(slots - 1, 0, -1):
        token_copy(slot, 0).start()
    fetch_down.wait()
    for bit in range(slots - 1):
        pick = jnp.int32(0)
        for slot in range(slots - 1):
            pick += jnp.where(bits[slot] == bit, slot + 1, 0)
        down_away[bit] = down_in[jnp.minimum(pick, slots - 1)]
    down[0, pl.ds(down_row, rows_down), :] = down_in[0]
    for slot in range(slots - 1, 0, -1):
        down_copy(slot).start()
    def make_hidden():
        mine.wait()
        for slot in range(1, slots):
            for half in (0, 1):
                token_copy(slot, half).wait_recv()

        def one(step, carry):
            half = (1 - x) * (1 - step) + x * step
            pre = jnp.dot(tok[0, half], up[0], preferred_element_type=jnp.float32)
            for slot in range(1, slots):
                pre += jnp.dot(tok[1 + bits[slot - 1], half], up[slot], preferred_element_type=jnp.float32)
            hid[0, half] = jax.nn.gelu(pre, approximate=True).astype(hid.dtype)
            return carry

        lax.fori_loop(0, 2, one, 0)
        for far in (1, 0):
            for slot in range(slots - 1, 0, -1):
                hid_copy(slot, far).start()

    def product(at, columns):
        total = jnp.dot(hid[0, at], down[0, :, columns], preferred_element_type=jnp.float32)
        for slot in range(1, slots):
            total += jnp.dot(hid[slot, at], down[slot, :, columns], preferred_element_type=jnp.float32)
        return total

    def make_away(i):
        unused, first, width = items[i]
        columns = slice(first, first + width)
        if first == 0:
            for slot in range(1, slots):
                hid_copy(slot, 1).wait_recv()
        stage[:, columns] = product(1 - x, columns).astype(stage.dtype)
        sum_copy(i).start()

    def complete(i):
        arrive(i, nz - 1)
        if i == 1:
            make_hidden()
        if i > 1:
            make_away(i)

    def first_send(i):
        if i >= count:
            return
        if i == 1:
            side(1 - x).wait_recv()
        if i == 2:
            for slot in range(1, slots):
                down_copy(slot).wait_recv()
        send(i, 1)

    count = len(items)
    for i in range(count):
        first_send(i + 1)
        for hop in range(1, nz):
            if hop < nz - 1:
                arrive(i, hop)
                send(i, hop + 1)
            if hop == 1 and i > 0:
                complete(i - 1)
        if i == 0:
            token_side().wait_recv()
            for slot in range(slots - 1, 0, -1):
                token_copy(slot, 1).start()
    complete(count - 1)
    for slot in range(1, slots):
        hid_copy(slot, 0).wait_recv()
    own[...] = product(x, slice(None))
    for i in range(2, count):
        sum_copy(i).wait_recv()
        columns = slice(items[i][1], items[i][1] + items[i][2])
        out_ref[:, columns] = (own[:, columns] + landed[:, columns].astype(jnp.float32)).astype(out_ref.dtype)

    side(x).wait_send()
    token_side().wait_send()
    for slot in range(1, slots):
        down_copy(slot).wait_send()
        for half in (0, 1):
            token_copy(slot, half).wait_send()
            hid_copy(slot, half).wait_send()
    for i in range(count):
        for hop in range(1, nz):
            sent(i, hop)
        if i > 1:
            sum_copy(i).wait_send()


def on_device(tokens, partner_bits, w_up, w_down):
    nz = lax.axis_size("dp") // 2
    slots = w_up.shape[1]
    rows, width = tokens.shape
    rows_up, hidden = w_up.shape[2], w_up.shape[3]
    rows_down = w_down.shape[2]
    half = hidden // 2
    items = item_list(width)
    count = len(items)
    kind = tokens.dtype
    dma = pltpu.SemaphoreType.DMA
    return pl.pallas_call(
        functools.partial(kernel, nz, items),
        out_shape=jax.ShapeDtypeStruct((rows, width), kind),
        in_specs=[pl.BlockSpec(memory_space=pltpu.SMEM)] + [pl.BlockSpec(memory_space=pl.ANY)] * 3,
        out_specs=pl.BlockSpec(memory_space=pltpu.VMEM),
        scratch_shapes=[
            pltpu.VMEM((slots, 2, rows, width), kind),
            pltpu.VMEM((slots, width, half), kind),
            pltpu.VMEM((slots, half, width), kind),
            pltpu.VMEM((slots, 2, rows, half), kind),
            pltpu.VMEM((rows, width), kind),
            pltpu.VMEM((rows, width), kind),
            pltpu.VMEM((rows, width), jnp.float32),
            pltpu.VMEM(w_up.shape[1:], kind),
            pltpu.VMEM(w_down.shape[1:], kind),
            pltpu.VMEM((slots, rows_up, half), kind),
            pltpu.VMEM((slots - 1,) + w_down.shape[2:], kind),
            dma((count, 2, nz - 1)),
            dma((count, 2, nz - 1)),
            dma((3,)),
            dma,
            dma,
            dma((slots, 2)),
            dma((slots, 2)),
            dma((slots,)),
            dma((slots,)),
            dma((slots, 2)),
            dma((slots, 2)),
            dma((count,)),
            dma((count,)),
        ],
        compiler_params=pltpu.CompilerParams(
            collective_id=0, has_side_effects=True, vmem_limit_bytes=67043328
        ),
    )(partner_bits.T, tokens, w_up, w_down)


def solution(mesh):
    in_specs = (
        P("dp", "tensor"),
        P(),
        P("tensor", None, "dp", None),
        P("tensor", None, "dp", None),
    )
    return jax.shard_map(
        on_device, mesh=mesh, in_specs=in_specs, out_specs=P("dp", "tensor"), check_vma=False
    )
```
